128 devices in a mesh: fsdp: 32 (over z, y, x_lo), sp: 4 (over x_hi, core).
Axes of the slice: x: 4 (x_hi: 2, x_lo: 2; x = x_hi * 2 + x_lo), y: 4, z: 4, core: 2. Of those that a mesh axis runs over, the one named last changes fastest.
Arguments:
- tokens: bfloat16 [32768, 768], P(('fsdp', 'sp')), may hold values from -60 to 60
- lengths: int32 [32], P('fsdp'), may hold values from 512 to 1024, as said below
- w_qkv: bfloat16 [768, 2304], P('fsdp'), may hold values from -0.21875 to 0.21875
- w_out: bfloat16 [768, 768], P('fsdp'), may hold values from -1.25 to 1.25
- w_in: bfloat16 [768, 3072], P('fsdp'), may hold values from -0.21875 to 0.21875
- w_back: bfloat16 [3072, 768], P('fsdp'), may hold values from -0.109375 to 0.109375
- bias_q: bfloat16 [768], P('fsdp'), may hold values from -3 to 3
- bias_v: bfloat16 [768], P('fsdp'), may hold values from -0.59765625 to 0.59765625
- bias_o: bfloat16 [768], P('fsdp'), may hold values from -3 to 3
- gain_one: bfloat16 [768], P('fsdp'), may hold values from 0.5 to 1.5
- shift_one: bfloat16 [768], P('fsdp'), may hold values from -3 to 3
- bias_in: bfloat16 [3072], P('fsdp'), may hold values from -3 to 3
- bias_back: bfloat16 [768], P('fsdp'), may hold values from -3 to 3
- gain_two: bfloat16 [768], P('fsdp'), may hold values from 0.5 to 1.5
- shift_two: bfloat16 [768], P('fsdp'), may hold values from -3 to 3
- cotangent: bfloat16 [32768, 768], P(('fsdp', 'sp')), may hold values from -24 to 24
Outputs:
- output: bfloat16 [32768, 768], P(('fsdp', 'sp'))
- grad_tokens: bfloat16 [32768, 768], P(('fsdp', 'sp'))
- grad_qkv: float32 [768, 2304], P('fsdp')
- grad_out: float32 [768, 768], P('fsdp')
- grad_in: float32 [768, 3072], P('fsdp')
- grad_back: float32 [3072, 768], P('fsdp')
- grad_bias_q: float32 [768], P('fsdp')
- grad_bias_v: float32 [768], P('fsdp')
- grad_bias_o: float32 [768], P('fsdp')
- grad_gain_one: float32 [768], P('fsdp')
- grad_shift_one: float32 [768], P('fsdp')
- grad_bias_in: float32 [3072], P('fsdp')
- grad_bias_back: float32 [768], P('fsdp')
- grad_gain_two: float32 [768], P('fsdp')
- grad_shift_two: float32 [768], P('fsdp')
The draws below stay inside these ranges and needn't reach their ends.
Inputs may be any that keep to these rules, and one draw needn't show every extreme that they name: `lengths`: each sequence's valid tokens are its first ones.
All inputs are finite; a program needn't handle non-finite values.
Results may differ from the reference program's by a relative error of at most 0.025.
The reference program's roundings to bfloat16 on the way count: a program that leaves them out, or rounds other values in their place, can miss the bound.
Values may be sent and summed in bfloat16 or wider, within the bound.
No kernel may reach another device: no remote copies, remote signals or barrier semaphores. Data moves between devices by JAX's collectives and lax.ppermute only.
A program may use at most 128 MiB of HBM per device.

```python
import jax
import jax.numpy as jnp
from jax import lax

H = 12
HD = 64
FF = 3072
D = 768
SEQ = 1024
SEQS = 32
TOKENS = 32768


def draw_tokens(key, part):
    base = jax.random.normal(key, (TOKENS, D), jnp.float32)
    return jnp.clip(base, -6.0, 6.0).astype(jnp.bfloat16)


def draw_lengths(key, part):
    lowest = SEQ // 2
    picked = jax.random.randint(key, (SEQS,), lowest, SEQ + 1, jnp.int32)
    order = jax.random.permutation(jax.random.fold_in(key, 3), SEQS)
    picked = picked.at[order[0]].set(SEQ)
    picked = picked.at[order[1]].set(lowest)
    return picked.astype(jnp.int32)


def raised(result, key, source, target, shards_of, factor):
    def block_of(dim):
        return (jnp.arange(result.shape[dim]) // (result.shape[dim] // shards_of)).reshape((-1,) + (1,) * (result.ndim - 1 - dim))

    one_side = jax.random.permutation(key, shards_of)[block_of(target)]
    far = (block_of(target) + shards_of // 2) % shards_of
    return jnp.where((block_of(source) == one_side) | (block_of(source) == far), factor * result, result)


def shard_levels(stream_key, extent, cuts, least, top_value):
    def one(axis_at, parts):
        draws = jax.random.uniform(jax.random.fold_in(jax.random.fold_in(stream_key, 6), axis_at), (parts,), jnp.float32, least / len(cuts), top_value / len(cuts))
        return jnp.repeat(jnp.exp(draws), extent[axis_at] // parts).reshape((-1,) + (1,) * (len(extent) - axis_at - 1))

    level = one(*cuts[0])
    for cut in cuts[1:]:
        level = level * one(*cut)
    return level


def bell_draw(key, extent, scale, most, cuts=(), kind=jnp.bfloat16):
    result = scale * jax.random.normal(key, extent, jnp.float32)
    if cuts:
        result = result * shard_levels(key, extent, cuts, -0.22, 0.18)
    return jnp.clip(result, -most, most).astype(kind)


def heavy_noise(stream_key, dims, scale, limit, cuts, heavy, kind=jnp.bfloat16):
    values = scale * jax.random.normal(stream_key, dims, jnp.float32)
    if cuts:
        values = values * shard_levels(stream_key, dims, cuts, -0.22, 0.18)
    return jnp.clip(raised(values, jax.random.fold_in(stream_key, 3), *heavy), -limit, limit).astype(kind)


def setup_inputs(seed: int = 0) -> dict:
    arg_keys = jax.random.split(jax.random.key(seed), 17)
    return {
        "tokens": draw_tokens(jax.random.fold_in(arg_keys[16], 71), 0),
        "lengths": draw_lengths(jax.random.fold_in(arg_keys[16], 71), 0),
        "w_qkv": bell_draw(arg_keys[2], (D, 3 * D), D ** -0.5, 0.21875, ((0, 32),)),
        "w_out": bell_draw(arg_keys[3], (D, D), (D // 32) ** -0.5, 1.25, ((0, 32),)),
        "w_in": bell_draw(arg_keys[4], (D, FF), D ** -0.5, 0.21875, ((0, 32),)),
        "w_back": bell_draw(arg_keys[5], (FF, D), FF ** -0.5, 0.109375, ((0, 32),)),
        "bias_q": bell_draw(arg_keys[6], (D,), 0.5, 3.0, ((0, 32),)),
        "bias_v": bell_draw(arg_keys[7], (D,), 0.1, 0.59765625, ((0, 32),)),
        "bias_o": bell_draw(arg_keys[8], (D,), 0.5, 3.0, ((0, 32),)),
        "gain_one": jnp.clip(1.0 + 0.1 * jax.random.normal(arg_keys[9], (D,), jnp.float32), 0.5, 1.5).astype(jnp.bfloat16),
        "shift_one": bell_draw(arg_keys[10], (D,), 0.5, 3.0, ((0, 32),)),
        "bias_in": bell_draw(arg_keys[11], (FF,), 0.5, 3.0, ((0, 32),)),
        "bias_back": bell_draw(arg_keys[12], (D,), 0.5, 3.0, ((0, 32),)),
        "gain_two": jnp.clip(1.0 + 0.1 * jax.random.normal(arg_keys[13], (D,), jnp.float32), 0.5, 1.5).astype(jnp.bfloat16),
        "shift_two": bell_draw(arg_keys[14], (D,), 0.5, 3.0, ((0, 32),)),
        "cotangent": heavy_noise(arg_keys[15], (TOKENS, D), 1.0, 24.0, ((0, 128),), (0, 1, 128, 5.5)),
    }


EPS = 1e-05

def layer_norm(hidden, gain, shift):
    mean = lax.optimization_barrier(jnp.mean(hidden, axis=-1, keepdims=True))
    centred = hidden - mean
    variance = lax.optimization_barrier(jnp.mean(centred * centred, axis=-1, keepdims=True))
    inverse = lax.rsqrt(variance + EPS)
    normed = centred * inverse
    return (normed * gain + shift, normed, inverse)

def norm_back(grad, normed, inverse, gain):
    scaled = grad * gain
    first = lax.optimization_barrier(jnp.mean(scaled, axis=-1, keepdims=True))
    second = lax.optimization_barrier(jnp.mean(scaled * normed, axis=-1, keepdims=True))
    return inverse * (scaled - first - normed * second)

def gelu_exact(value):
    return jax.nn.gelu(value, approximate=False)

def rounded(value):
    return lax.optimization_barrier(value.astype(jnp.bfloat16)).astype(jnp.float32)

def attend(query, keys, values, valid, scale):
    total = query.shape[0]
    block = min(512, total)
    count = total // block
    qf = query.astype(jnp.float32)
    kf = keys.astype(jnp.float32)
    vf = values.astype(jnp.float32)

    def one(index):
        rows = lax.dynamic_slice_in_dim(qf, index * block, block, 0)
        scores = jnp.einsum('qhd,khd->hqk', rows, kf) * scale
        scores = jnp.where(valid[None, None, :], scores, -jnp.inf)
        top = lax.optimization_barrier(jnp.max(scores, axis=-1, keepdims=True))
        expo = jnp.exp(scores - top)
        summed = lax.optimization_barrier(jnp.sum(expo, axis=-1, keepdims=True))
        probs = rounded(expo / summed)
        context = jnp.einsum('hqk,khd->qhd', probs, vf).astype(jnp.bfloat16)
        return (context, (top + jnp.log(summed))[..., 0])
    context, logsum = lax.map(one, jnp.arange(count, dtype=jnp.int32))
    return (context.reshape(query.shape), logsum)

def attend_back(query, keys, values, context, logsum, grad_context, valid, scale):
    total = query.shape[0]
    block = min(512, total)
    count = total // block
    qf = query.astype(jnp.float32)
    kf = keys.astype(jnp.float32)
    vf = values.astype(jnp.float32)
    of = context.astype(jnp.float32)
    gf = grad_context.astype(jnp.float32)

    def one(carry, index):
        grad_keys, grad_values = carry
        rows = lax.dynamic_slice_in_dim(qf, index * block, block, 0)
        outs = lax.dynamic_slice_in_dim(of, index * block, block, 0)
        grads = lax.dynamic_slice_in_dim(gf, index * block, block, 0)
        logs = logsum[index]
        scores = jnp.einsum('qhd,khd->hqk', rows, kf) * scale
        scores = jnp.where(valid[None, None, :], scores, -jnp.inf)
        probs = jnp.exp(scores - logs[..., None])
        probs_r = rounded(probs)
        grad_values = grad_values + jnp.einsum('hqk,qhd->khd', probs_r, grads)
        grad_probs = jnp.einsum('qhd,khd->hqk', grads, vf)
        delta = lax.optimization_barrier(jnp.sum(grads * outs, axis=-1)).T
        grad_scores = rounded(probs * (grad_probs - delta[..., None]))
        grad_rows = (jnp.einsum('hqk,khd->qhd', grad_scores, kf) * scale).astype(jnp.bfloat16)
        grad_keys = grad_keys + jnp.einsum('hqk,qhd->khd', grad_scores, rows) * scale
        return ((grad_keys, grad_values), grad_rows)
    zero = jnp.zeros(query.shape, jnp.float32)
    (grad_keys, grad_values), grad_query = lax.scan(one, (zero, zero), jnp.arange(count, dtype=jnp.int32))
    return (grad_query.reshape(query.shape), grad_keys.astype(jnp.bfloat16), grad_values.astype(jnp.bfloat16))

def reference(tokens, lengths, w_qkv, w_out, w_in, w_back, bias_q, bias_v, bias_o, gain_one, shift_one, bias_in, bias_back, gain_two, shift_two, cotangent):
    width = H * HD
    scale = HD ** (-0.5)
    f32 = jnp.float32
    bias_qkv = jnp.concatenate([bias_q.astype(f32), jnp.zeros((width,), f32), bias_v.astype(f32)])
    b_o = bias_o.astype(f32)
    g_one = gain_one.astype(f32)
    s_one = shift_one.astype(f32)
    b_in = bias_in.astype(f32)
    b_back = bias_back.astype(f32)
    g_two = gain_two.astype(f32)
    s_two = shift_two.astype(f32)

    def one_sequence(carry, item):
        x, cot, length = item
        valid = jnp.arange(SEQ, dtype=jnp.int32) < length
        packed = (jnp.dot(x, w_qkv, preferred_element_type=f32) + bias_qkv).astype(jnp.bfloat16)
        query = packed[:, :width].reshape(SEQ, H, HD)
        keys = packed[:, width:2 * width].reshape(SEQ, H, HD)
        values = packed[:, 2 * width:].reshape(SEQ, H, HD)
        context, logsum = attend(query, keys, values, valid, scale)
        ctx_rows = context.reshape(SEQ, width)
        h_one = x.astype(f32) + jnp.dot(ctx_rows, w_out, preferred_element_type=f32) + b_o
        y_one, n_one, i_one = layer_norm(h_one, g_one, s_one)
        y_oneb = y_one.astype(jnp.bfloat16)
        pre = jnp.dot(y_oneb, w_in, preferred_element_type=f32) + b_in
        act = gelu_exact(pre).astype(jnp.bfloat16)
        h_two = y_oneb.astype(f32) + jnp.dot(act, w_back, preferred_element_type=f32) + b_back
        out, n_two, i_two = layer_norm(h_two, g_two, s_two)
        grad = cot.astype(f32)
        d_g2 = lax.optimization_barrier(jnp.sum(grad * n_two, axis=0))
        d_s2 = lax.optimization_barrier(jnp.sum(grad, axis=0))
        dh_two = norm_back(grad, n_two, i_two, g_two)
        d_bb = lax.optimization_barrier(jnp.sum(dh_two, axis=0))
        dh_twob = dh_two.astype(jnp.bfloat16)
        d_wb = jnp.dot(act.T, dh_twob, preferred_element_type=f32)
        d_act = jnp.dot(dh_twob, w_back.T, preferred_element_type=f32)
        d_pre = jax.vjp(gelu_exact, pre)[1](d_act)[0]
        d_bi = lax.optimization_barrier(jnp.sum(d_pre, axis=0))
        d_preb = d_pre.astype(jnp.bfloat16)
        d_wi = jnp.dot(y_oneb.T, d_preb, preferred_element_type=f32)
        dy_one = dh_two + jnp.dot(d_preb, w_in.T, preferred_element_type=f32)
        d_g1 = lax.optimization_barrier(jnp.sum(dy_one * n_one, axis=0))
        d_s1 = lax.optimization_barrier(jnp.sum(dy_one, axis=0))
        dh_one = norm_back(dy_one, n_one, i_one, g_one)
        d_bo = lax.optimization_barrier(jnp.sum(dh_one, axis=0))
        dh_oneb = dh_one.astype(jnp.bfloat16)
        d_wo = jnp.dot(ctx_rows.T, dh_oneb, preferred_element_type=f32)
        d_ctx = jnp.dot(dh_oneb, w_out.T, preferred_element_type=f32).astype(jnp.bfloat16).reshape(SEQ, H, HD)
        g_query, g_keys, g_values = attend_back(query, keys, values, context, logsum, d_ctx, valid, scale)
        d_packed = jnp.concatenate([g_query.reshape(SEQ, width), g_keys.reshape(SEQ, width), g_values.reshape(SEQ, width)], axis=1)
        d_bq = lax.optimization_barrier(jnp.sum(g_query.reshape(SEQ, width).astype(f32), axis=0))
        d_bv = lax.optimization_barrier(jnp.sum(g_values.reshape(SEQ, width).astype(f32), axis=0))
        d_wq = jnp.dot(x.T, d_packed, preferred_element_type=f32)
        d_x = (dh_one + jnp.dot(d_packed, w_qkv.T, preferred_element_type=f32)).astype(jnp.bfloat16)
        terms = (d_wq, d_wo, d_wi, d_wb, d_bq, d_bv, d_bo, d_g1, d_s1, d_bi, d_bb, d_g2, d_s2)
        carry = tuple((a + b for a, b in zip(carry, terms)))
        return (carry, (out.astype(jnp.bfloat16), d_x))
    start = (jnp.zeros((width, 3 * width), f32), jnp.zeros((width, width), f32), jnp.zeros((width, FF), f32), jnp.zeros((FF, width), f32), jnp.zeros((width,), f32), jnp.zeros((width,), f32), jnp.zeros((width,), f32), jnp.zeros((width,), f32), jnp.zeros((width,), f32), jnp.zeros((FF,), f32), jnp.zeros((width,), f32), jnp.zeros((width,), f32), jnp.zeros((width,), f32))
    items = (tokens.reshape(SEQS, SEQ, width), cotangent.reshape(SEQS, SEQ, width), lengths.astype(jnp.int32))
    grads, (outs, d_xs) = lax.scan(one_sequence, start, items)
    return (outs.reshape(TOKENS, width), d_xs.reshape(TOKENS, width), grads[0], grads[1], grads[2], grads[3], grads[4], grads[5], grads[6], grads[7], grads[8], grads[9], grads[10], grads[11], grads[12])
```

```python
import jax
import jax.numpy as jnp
from jax import lax
from jax.sharding import Mesh
from jax.sharding import PartitionSpec as P

H = 12
HD = 64
FSDP = "fsdp"
SP = ("sp_0", "sp_1")
FSDP_SP = ("fsdp", "sp_0", "sp_1")
EPS = 1e-05
BF = jnp.bfloat16
F32 = jnp.float32


def swap_core(value):
    return lax.ppermute(value, "sp_1", [(0, 1), (1, 0)])


def swap_chip(value):
    return lax.ppermute(value, "sp_0", [(0, 1), (1, 0)])


def swap_both(value):
    return lax.ppermute(value, SP, [(0, 3), (1, 2), (2, 1), (3, 0)])


def gather_relative(value):
    across = swap_chip(value)
    return [value, swap_core(value), across, swap_core(across)]


def gather_direct(value):
    return [value, swap_core(value), swap_chip(value), swap_both(value)]


def exchange_direct(parts):
    return [parts[0], swap_core(parts[1]), swap_chip(parts[2]), swap_both(parts[3])]


def reduce_relative(parts):
    far = parts[2] + swap_core(parts[3].astype(BF)).astype(F32)
    far = swap_chip(far.astype(BF)).astype(F32)
    near = parts[0] + swap_core(parts[1].astype(BF)).astype(F32)
    return near + far


def reorder(parts):
    chip = lax.axis_index("sp_0") == 1
    core = lax.axis_index("sp_1") == 1
    a, b, c, d = parts
    a, b, c, d = (
        jnp.where(core, b, a),
        jnp.where(core, a, b),
        jnp.where(core, d, c),
        jnp.where(core, c, d),
    )
    return [
        jnp.where(chip, c, a),
        jnp.where(chip, d, b),
        jnp.where(chip, a, c),
        jnp.where(chip, b, d),
    ]


def spread(value):
    copies = jnp.broadcast_to(value, (lax.axis_size(FSDP), *value.shape))
    filled = lax.all_to_all(copies, FSDP, split_axis=0, concat_axis=0, tiled=True)
    return filled.reshape(-1, value.shape[-1])


def collect(value):
    count = lax.axis_size(FSDP)
    blocks = value.reshape(count, value.shape[0] // count, value.shape[1])
    blocks = lax.all_to_all(blocks, FSDP, split_axis=0, concat_axis=0, tiled=True)
    return blocks.astype(F32).sum(axis=0)


def layer_norm(hidden, gain, shift):
    mean = jnp.mean(hidden, axis=-1, keepdims=True)
    centred = hidden - mean
    variance = jnp.mean(centred * centred, axis=-1, keepdims=True)
    inverse = lax.rsqrt(variance + EPS)
    normed = centred * inverse
    return (normed * gain + shift, normed, inverse)


def norm_back(grad, normed, inverse, gain):
    scaled = grad * gain
    first = jnp.mean(scaled, axis=-1, keepdims=True)
    second = jnp.mean(scaled * normed, axis=-1, keepdims=True)
    return inverse * (scaled - first - normed * second)


def gelu_exact(value):
    return jax.nn.gelu(value, approximate=False)


def dot(left, right):
    return jnp.dot(left, right, preferred_element_type=F32)


def contract_rows(left, right):
    return lax.dot_general(left, right, (((0,), (0,)), ((), ())), preferred_element_type=F32)


def contract_cols(left, right):
    return lax.dot_general(left, right, (((1,), (1,)), ((), ())), preferred_element_type=F32)


def attend_heads(query, keys, values, valid, scale):
    scores = jnp.einsum("qhd,khd->hqk", query, keys, preferred_element_type=F32) * scale
    scores = jnp.where(valid[None, None, :], scores, -jnp.inf)
    top = jnp.max(scores, axis=-1, keepdims=True)
    expo = jnp.exp(scores - top)
    summed = jnp.sum(expo, axis=-1, keepdims=True)
    probs = (expo / summed).astype(BF)
    context = jnp.einsum("hqk,khd->qhd", probs, values, preferred_element_type=F32).astype(BF)
    return (context, (top + jnp.log(summed))[..., 0])


def attend_back(query, keys, values, context, logsum, grads, valid, scale):
    scores = jnp.einsum("qhd,khd->hqk", query, keys, preferred_element_type=F32) * scale
    scores = jnp.where(valid[None, None, :], scores, -jnp.inf)
    probs = jnp.exp(scores - logsum[..., None])
    probs_b = probs.astype(BF)
    grad_values = jnp.einsum("hqk,qhd->khd", probs_b, grads, preferred_element_type=F32)
    grad_probs = jnp.einsum("qhd,khd->hqk", grads, values, preferred_element_type=F32)
    delta = jnp.sum(grads.astype(F32) * context.astype(F32), axis=-1).T
    grad_scores = (probs * (grad_probs - delta[..., None])).astype(BF)
    grad_query = jnp.einsum("hqk,khd->qhd", grad_scores, keys, preferred_element_type=F32) * scale
    grad_keys = jnp.einsum("hqk,qhd->khd", grad_scores, query, preferred_element_type=F32) * scale
    return (grad_query.astype(BF), grad_keys.astype(BF), grad_values.astype(BF))


def body(
    tokens,
    lengths,
    w_qkv,
    w_out,
    w_in,
    w_back,
    bias_q,
    bias_v,
    bias_o,
    gain_one,
    shift_one,
    bias_in,
    bias_back,
    gain_two,
    shift_two,
    cotangent,
):
    rows, width = tokens.shape
    members = lax.axis_size(SP)
    shards = lax.axis_size(FSDP)
    local = H // members
    span = local * HD
    total = rows * members
    scale = HD ** (-0.5)
    depth = w_qkv.shape[0]
    piece = w_back.shape[0] // members
    hidden = piece * shards
    me = lax.axis_index("sp_0") * 2 + lax.axis_index("sp_1")

    mine_qkv = lax.dynamic_index_in_dim(w_qkv.reshape(depth, 3, members, span), me, 2, False)
    mine_in = lax.dynamic_index_in_dim(w_in.reshape(depth, shards, members, piece), me, 2, False)
    mine_back = lax.dynamic_index_in_dim(w_back.reshape(members, piece, width), me, 0, False)
    mine_bias = lax.dynamic_index_in_dim(bias_in.reshape(members, piece), me, 0, False)
    vectors = jnp.stack(
        [bias_q, bias_v, bias_o, gain_one, shift_one, bias_back, gain_two, shift_two, mine_bias],
        axis=1,
    )
    vectors = jnp.pad(vectors, ((0, 0), (0, 64 - vectors.shape[1])))
    first = spread(jnp.concatenate([mine_qkv.reshape(depth, 3 * span), vectors], axis=1))
    second = spread(
        jnp.concatenate([w_out, mine_in.reshape(depth, hidden), mine_back], axis=1)
    )
    w_qkv_m = first[:, : 3 * span]
    small = first[:, 3 * span :].astype(F32).T
    b_q, b_v, b_o, g_one, s_one, b_back, g_two, s_two, b_in = [small[k] for k in range(9)]
    w_out_all = second[:, :width]
    w_in_m = second[:, width : width + hidden]
    w_back_m = second[:, width + hidden :]

    x_all = jnp.concatenate(gather_relative(tokens), axis=0)
    own_q = lax.dynamic_slice_in_dim(b_q, me * span, span, 0)
    own_v = lax.dynamic_slice_in_dim(b_v, me * span, span, 0)
    bias_qkv = jnp.concatenate([own_q, jnp.zeros((span,), F32), own_v])
    packed = (dot(x_all, w_qkv_m) + bias_qkv).astype(BF)
    query, keys, values = [
        packed[:, k * span : (k + 1) * span].reshape(total, local, HD) for k in range(3)
    ]
    place = jnp.arange(members, dtype=jnp.int32) ^ me
    position = (place[:, None] * rows + jnp.arange(rows, dtype=jnp.int32)).reshape(total)
    valid = position < lengths[0]
    context, logsum = attend_heads(query, keys, values, valid, scale)

    parts = context.reshape(members, rows, span)
    ctx_rows = jnp.concatenate(
        reorder(exchange_direct([parts[m] for m in range(members)])), axis=1
    )
    h_one = tokens.astype(F32) + dot(ctx_rows, w_out_all) + b_o
    y_one, n_one, i_one = layer_norm(h_one, g_one, s_one)
    y_oneb = y_one.astype(BF)
    y_all = jnp.concatenate(gather_relative(y_oneb), axis=0)
    pre = dot(y_all, w_in_m) + b_in
    act = gelu_exact(pre).astype(BF)
    partial = dot(act, w_back_m).reshape(members, rows, width)
    h_two = y_oneb.astype(F32) + b_back + reduce_relative(partial)
    out, n_two, i_two = layer_norm(h_two, g_two, s_two)

    grad = cotangent.astype(F32)
    d_g2 = jnp.sum(grad * n_two, axis=0)
    d_s2 = jnp.sum(grad, axis=0)
    dh_two = norm_back(grad, n_two, i_two, g_two)
    d_bb = jnp.sum(dh_two, axis=0)
    dh_all = jnp.concatenate(gather_relative(dh_two.astype(BF)), axis=0)
    d_act = contract_cols(dh_all, w_back_m)
    d_pre = jax.vjp(gelu_exact, pre)[1](d_act)[0]
    d_preb = d_pre.astype(BF)
    back = contract_cols(d_preb, w_in_m).reshape(members, rows, width)
    dy_one = dh_two + reduce_relative(back)
    d_bi = jnp.sum(d_pre, axis=0)
    d_wb = contract_rows(act, dh_all)
    d_wi = contract_rows(y_all, d_preb)

    d_g1 = jnp.sum(dy_one * n_one, axis=0)
    d_s1 = jnp.sum(dy_one, axis=0)
    dh_one = norm_back(dy_one, n_one, i_one, g_one)
    d_bo = jnp.sum(dh_one, axis=0)
    dh_oneb = dh_one.astype(BF)
    d_ctx = contract_cols(dh_oneb, w_out_all).astype(BF)
    pieces = exchange_direct(reorder([d_ctx[:, m * span : (m + 1) * span] for m in range(members)]))
    grad_heads = jnp.concatenate(pieces, axis=0).reshape(total, local, HD)

    columns = reorder([dh_oneb[:, m * span : (m + 1) * span] for m in range(members)])
    d_wo = reduce_relative([contract_rows(ctx_rows, column) for column in columns])
    early = collect(jnp.concatenate([d_wo.astype(BF), d_wi.astype(BF), d_wb.astype(BF)], axis=1))
    early = reorder(gather_direct(early))

    g_query, g_keys, g_values = attend_back(
        query, keys, values, context, logsum, grad_heads, valid, scale
    )
    d_packed = jnp.concatenate(
        [g.reshape(total, span) for g in (g_query, g_keys, g_values)], axis=1
    )
    d_x = dh_one + reduce_relative(contract_cols(d_packed, w_qkv_m).reshape(members, rows, width))
    d_wq = contract_rows(x_all, d_packed)
    empty = jnp.zeros((width,), F32)
    own = jnp.sum(d_packed.astype(F32), axis=0)
    d_bq = lax.dynamic_update_slice_in_dim(empty, own[:span], me * span, 0)
    d_bv = lax.dynamic_update_slice_in_dim(empty, own[2 * span :], me * span, 0)
    sums = jnp.stack([d_bq, d_bv, d_bo, d_g1, d_s1, d_bb, d_g2, d_s2, d_bi], axis=1)
    sums = jnp.pad(sums, ((0, 0), (0, 64 - sums.shape[1])))
    late = collect(jnp.concatenate([d_wq, sums], axis=1).astype(BF))
    late = reorder(gather_direct(late))

    grad_qkv = (
        jnp.stack([part[:, : 3 * span].reshape(depth, 3, span) for part in late], axis=2)
    ).reshape(depth, 3 * width)
    grad_out = jnp.concatenate([part[:, :span] for part in early], axis=1)
    grad_in = jnp.stack(
        [part[:, span : span + hidden].reshape(depth, shards, piece) for part in early], axis=2
    ).reshape(depth, members * hidden)
    grad_back = jnp.concatenate([part[:, span + hidden :] for part in early], axis=0)
    tails = [part[:, 3 * span : 3 * span + 9].T for part in late]
    summed = tails[0] + tails[1] + tails[2] + tails[3]
    grad_bias_in = jnp.concatenate([tail[8] for tail in tails])
    return (
        out.astype(BF),
        d_x.astype(BF),
        grad_qkv,
        grad_out,
        grad_in,
        grad_back,
        summed[0],
        summed[1],
        summed[2],
        summed[3],
        summed[4],
        grad_bias_in,
        summed[5],
        summed[6],
        summed[7],
    )


def solution(mesh):
    split = Mesh(mesh.devices.reshape(mesh.shape["fsdp"], 2, 2), FSDP_SP)
    rows, flat = P("fsdp", None), P("fsdp")
    both = P(FSDP_SP, None)
    in_specs = (both, flat, rows, rows, rows, rows, *(flat,) * 9, both)
    out_specs = (both, both, rows, rows, rows, rows, *(flat,) * 9)
    return jax.shard_map(body, mesh=split, in_specs=in_specs, out_specs=out_specs, check_vma=False)
```

```python
import jax
import jax.numpy as jnp
from jax import lax
from jax.sharding import Mesh
from jax.sharding import PartitionSpec as P

H = 12
HD = 64
FSDP = ("plane", "pair")
SP = ("sp_0", "sp_1")
FSDP_SP = ("plane", "pair", "sp_0", "sp_1")
EPS = 1e-05
BF = jnp.bfloat16
F32 = jnp.float32


def swap_core(value):
    return lax.ppermute(value, "sp_1", [(0, 1), (1, 0)])


def swap_chip(value):
    return lax.ppermute(value, "sp_0", [(0, 1), (1, 0)])


def swap_both(value):
    return lax.ppermute(value, SP, [(0, 3), (1, 2), (2, 1), (3, 0)])


def swap_pair(value):
    return lax.ppermute(value, "pair", [(0, 1), (1, 0)])


def gather_direct(value):
    return [value, swap_core(value), swap_chip(value), swap_both(value)]


def gather_halves(value):
    across = swap_chip(value)
    near = jnp.concatenate([value, swap_core(value)], axis=0)
    return near, jnp.concatenate([across, swap_core(across)], axis=0)


def send_half(half):
    rows = half.shape[0] // 2
    return half[:rows] + swap_core(half[rows:].astype(BF)).astype(F32)


def reduce_far(far):
    return swap_chip(send_half(far).astype(BF)).astype(F32)


def reorder(parts):
    chip = lax.axis_index("sp_0") == 1
    core = lax.axis_index("sp_1") == 1
    a, b, c, d = parts
    a, b, c, d = (
        jnp.where(core, b, a),
        jnp.where(core, a, b),
        jnp.where(core, d, c),
        jnp.where(core, c, d),
    )
    return [
        jnp.where(chip, c, a),
        jnp.where(chip, d, b),
        jnp.where(chip, a, c),
        jnp.where(chip, b, d),
    ]


def spread(value):
    copies = jnp.broadcast_to(value, (lax.axis_size(FSDP), *value.shape))
    filled = lax.all_to_all(copies, FSDP, split_axis=0, concat_axis=0, tiled=True)
    return filled.reshape(-1, value.shape[-1])


def spread_pairs(value):
    other = swap_pair(value)
    high = lax.axis_index("pair") == 1
    both = jnp.stack([jnp.where(high, other, value), jnp.where(high, value, other)], axis=1)
    copies = jnp.broadcast_to(both, (lax.axis_size("plane"), *both.shape))
    filled = lax.all_to_all(copies, "plane", split_axis=0, concat_axis=0, tiled=True)
    return [filled[:, k].reshape(-1, value.shape[-1]) for k in range(value.shape[0])]


def collect(values):
    count = lax.axis_size("plane")
    blocks = jnp.stack([v.reshape(count, 2, -1, v.shape[-1]) for v in values], axis=2)
    blocks = lax.all_to_all(blocks, "plane", split_axis=0, concat_axis=0, tiled=True)
    summed = blocks.astype(F32).sum(axis=0)
    high = lax.axis_index("pair") == 1
    keep = jnp.where(high, summed[1], summed[0])
    return keep + swap_pair(jnp.where(high, summed[0], summed[1]))


def layer_norm(hidden, gain, shift):
    mean = jnp.mean(hidden, axis=-1, keepdims=True)
    centred = hidden - mean
    variance = jnp.mean(centred * centred, axis=-1, keepdims=True)
    inverse = lax.rsqrt(variance + EPS)
    normed = centred * inverse
    return (normed * gain + shift, normed, inverse)


def norm_back(grad, normed, inverse, gain):
    scaled = grad * gain
    first = jnp.mean(scaled, axis=-1, keepdims=True)
    second = jnp.mean(scaled * normed, axis=-1, keepdims=True)
    return inverse * (scaled - first - normed * second)


def gelu_exact(value):
    return jax.nn.gelu(value, approximate=False)


def dot(left, right):
    return jnp.dot(left, right, preferred_element_type=F32)


def contract_rows(left, right):
    return lax.dot_general(left, right, (((0,), (0,)), ((), ())), preferred_element_type=F32)


def contract_cols(left, right):
    return lax.dot_general(left, right, (((1,), (1,)), ((), ())), preferred_element_type=F32)


def attend_heads(query, keys, values, valid, scale):
    scores = jnp.einsum("qhd,khd->hqk", query, keys, preferred_element_type=F32) * scale
    scores = jnp.where(valid[None, None, :], scores, -jnp.inf)
    top = jnp.max(scores, axis=-1, keepdims=True)
    expo = jnp.exp(scores - top)
    summed = jnp.sum(expo, axis=-1, keepdims=True)
    probs = (expo / summed).astype(BF)
    context = jnp.einsum("hqk,khd->qhd", probs, values, preferred_element_type=F32).astype(BF)
    return (context, (top + jnp.log(summed))[..., 0])


def attend_back(query, keys, values, context, logsum, grads, valid, scale):
    scores = jnp.einsum("qhd,khd->hqk", query, keys, preferred_element_type=F32) * scale
    scores = jnp.where(valid[None, None, :], scores, -jnp.inf)
    probs = jnp.exp(scores - logsum[..., None])
    probs_b = probs.astype(BF)
    grad_values = jnp.einsum("hqk,qhd->khd", probs_b, grads, preferred_element_type=F32)
    grad_probs = jnp.einsum("qhd,khd->hqk", grads, values, preferred_element_type=F32)
    delta = jnp.sum(grads.astype(F32) * context.astype(F32), axis=-1).T
    grad_scores = (probs * (grad_probs - delta[..., None])).astype(BF)
    grad_query = jnp.einsum("hqk,khd->qhd", grad_scores, keys, preferred_element_type=F32) * scale
    grad_keys = jnp.einsum("hqk,qhd->khd", grad_scores, query, preferred_element_type=F32) * scale
    return (grad_query.astype(BF), grad_keys.astype(BF), grad_values.astype(BF))


def body(
    tokens,
    lengths,
    w_qkv,
    w_out,
    w_in,
    w_back,
    bias_q,
    bias_v,
    bias_o,
    gain_one,
    shift_one,
    bias_in,
    bias_back,
    gain_two,
    shift_two,
    cotangent,
):
    rows, width = tokens.shape
    members = lax.axis_size(SP)
    shards = lax.axis_size(FSDP)
    local = H // members
    span = local * HD
    total = rows * members
    scale = HD ** (-0.5)
    depth = w_qkv.shape[0]
    piece = w_back.shape[0] // members
    hidden = piece * shards
    me = lax.axis_index("sp_0") * 2 + lax.axis_index("sp_1")

    mine_qkv = lax.dynamic_index_in_dim(w_qkv.reshape(depth, 3, members, span), me, 2, False)
    mine_out = lax.dynamic_slice_in_dim(w_out, me * span, span, 1)
    mine_in = lax.dynamic_index_in_dim(w_in.reshape(depth, shards, members, piece), me, 2, False)
    mine_back = lax.dynamic_index_in_dim(w_back.reshape(members, piece, width), me, 0, False)
    mine_bias = lax.dynamic_index_in_dim(bias_in.reshape(members, piece), me, 0, False)
    vectors = jnp.stack(
        [bias_q, bias_v, bias_o, gain_one, shift_one, bias_back, gain_two, shift_two, mine_bias],
        axis=1,
    )
    vectors = jnp.pad(vectors, ((0, 0), (0, 128 - vectors.shape[1])))
    first = spread(jnp.concatenate([mine_qkv.reshape(depth, 3 * span), mine_out, vectors], axis=1))
    w_in_m, w_back_m = spread_pairs(jnp.stack([mine_in.reshape(depth, hidden), mine_back]))
    w_qkv_m = first[:, : 3 * span]
    w_out_m = first[:, 3 * span : 4 * span]
    small = first[:, 4 * span :].astype(F32).T
    b_q, b_v, b_o, g_one, s_one, b_back, g_two, s_two, b_in = [small[k] for k in range(9)]
    w_out_all = jnp.concatenate(reorder(gather_direct(w_out_m)), axis=1)

    x_near, x_far = gather_halves(tokens)
    x_all = jnp.concatenate([x_near, x_far], axis=0)
    own_q = lax.dynamic_slice_in_dim(b_q, me * span, span, 0)
    own_v = lax.dynamic_slice_in_dim(b_v, me * span, span, 0)
    bias_qkv = jnp.concatenate([own_q, jnp.zeros((span,), F32), own_v])
    packed = (dot(x_all, w_qkv_m) + bias_qkv).astype(BF)
    query, keys, values = [
        packed[:, k * span : (k + 1) * span].reshape(total, local, HD) for k in range(3)
    ]
    place = jnp.arange(members, dtype=jnp.int32) ^ me
    position = (place[:, None] * rows + jnp.arange(rows, dtype=jnp.int32)).reshape(total)
    valid = position < lengths[0]
    half = total // 2
    context_far, logsum_far = attend_heads(query[half:], keys, values, valid, scale)
    far = context_far.reshape(2, rows, span)
    far = [swap_chip(far[0]), swap_both(far[1])]
    context_near, logsum_near = attend_heads(query[:half], keys, values, valid, scale)
    near = context_near.reshape(2, rows, span)
    ctx_rows = jnp.concatenate(reorder([near[0], swap_core(near[1]), *far]), axis=1)
    h_one = tokens.astype(F32) + dot(ctx_rows, w_out_all) + b_o
    y_one, n_one, i_one = layer_norm(h_one, g_one, s_one)
    y_oneb = y_one.astype(BF)

    def forward(y):
        pre = dot(y, w_in_m) + b_in
        act = gelu_exact(pre).astype(BF)
        return pre, act, dot(act, w_back_m)

    y_near, y_far = gather_halves(y_oneb)
    pre_near, act_near, partial_near = forward(y_near)
    pre_far, act_far, partial_far = forward(y_far)
    h_two = y_oneb.astype(F32) + b_back + send_half(partial_near) + reduce_far(partial_far)
    out, n_two, i_two = layer_norm(h_two, g_two, s_two)

    grad = cotangent.astype(F32)
    d_g2 = jnp.sum(grad * n_two, axis=0)
    d_s2 = jnp.sum(grad, axis=0)
    dh_two = norm_back(grad, n_two, i_two, g_two)
    d_bb = jnp.sum(dh_two, axis=0)

    def backward(dh, pre):
        d_pre = jax.vjp(gelu_exact, pre)[1](contract_cols(dh, w_back_m))[0]
        d_preb = d_pre.astype(BF)
        return d_preb, jnp.sum(d_pre, axis=0), contract_cols(d_preb, w_in_m)

    dh_near, dh_far = gather_halves(dh_two.astype(BF))
    d_pre_near, d_bi_near, back_near = backward(dh_near, pre_near)
    d_pre_far, d_bi_far, back_far = backward(dh_far, pre_far)
    dy_one = dh_two + send_half(back_near) + reduce_far(back_far)
    d_bi = d_bi_near + d_bi_far
    d_wb = (contract_rows(act_near, dh_near) + contract_rows(act_far, dh_far)).astype(BF)
    d_wi = (contract_rows(y_near, d_pre_near) + contract_rows(y_far, d_pre_far)).astype(BF)
    d_wi, d_wb, dy_one = lax.optimization_barrier((d_wi, d_wb, dy_one))
    early = collect([d_wi, d_wb])
    early = reorder(gather_direct(early))

    d_g1 = jnp.sum(dy_one * n_one, axis=0)
    d_s1 = jnp.sum(dy_one, axis=0)
    dh_one = norm_back(dy_one, n_one, i_one, g_one)
    d_bo = jnp.sum(dh_one, axis=0)
    dh_oneb = dh_one.astype(BF)
    d_ctx = contract_cols(dh_oneb, w_out_all).astype(BF)
    pieces = reorder([d_ctx[:, m * span : (m + 1) * span] for m in range(members)])
    pieces = [pieces[0], swap_core(pieces[1]), swap_chip(pieces[2]), swap_both(pieces[3])]
    grad_heads = jnp.concatenate(pieces, axis=0).reshape(total, local, HD)

    columns = reorder([dh_oneb[:, m * span : (m + 1) * span] for m in range(members)])
    d_wo = [contract_rows(ctx_rows, column) for column in columns]
    d_wo_far = reduce_far(jnp.concatenate(d_wo[2:], axis=0))
    d_wo = send_half(jnp.concatenate(d_wo[:2], axis=0)) + d_wo_far

    context = jnp.concatenate([context_near, context_far], axis=0)
    logsum = jnp.concatenate([logsum_near, logsum_far], axis=1)
    g_query, g_keys, g_values = attend_back(
        query, keys, values, context, logsum, grad_heads, valid, scale
    )
    d_packed = jnp.concatenate(
        [g.reshape(total, span) for g in (g_query, g_keys, g_values)], axis=1
    )
    d_x_far = reduce_far(contract_cols(d_packed[half:], w_qkv_m))
    d_x = dh_one + send_half(contract_cols(d_packed[:half], w_qkv_m)) + d_x_far
    d_wq = contract_rows(x_all, d_packed)
    empty = jnp.zeros((width,), F32)
    own = jnp.sum(d_packed.astype(F32), axis=0)
    d_bq = lax.dynamic_update_slice_in_dim(empty, own[:span], me * span, 0)
    d_bv = lax.dynamic_update_slice_in_dim(empty, own[2 * span :], me * span, 0)
    sums = jnp.stack([d_bq, d_bv, d_bo, d_g1, d_s1, d_bb, d_g2, d_s2, d_bi], axis=1)
    sums = jnp.pad(sums, ((0, 0), (0, 128 - sums.shape[1])))
    late = collect([jnp.concatenate([d_wq, d_wo, sums], axis=1).astype(BF)])[0]
    late = reorder(gather_direct(late))

    grad_qkv = (
        jnp.stack([part[:, : 3 * span].reshape(depth, 3, span) for part in late], axis=2)
    ).reshape(depth, 3 * width)
    grad_out = jnp.concatenate([part[:, 3 * span : 4 * span] for part in late], axis=1)
    grad_in = jnp.stack([part[0].reshape(depth, shards, piece) for part in early], axis=2).reshape(
        depth, members * hidden
    )
    grad_back = jnp.concatenate([part[1] for part in early], axis=0)
    tails = [part[:, 4 * span : 4 * span + 9].T for part in late]
    summed = tails[0] + tails[1] + tails[2] + tails[3]
    grad_bias_in = jnp.concatenate([tail[8] for tail in tails])
    return (
        out.astype(BF),
        d_x.astype(BF),
        grad_qkv,
        grad_out,
        grad_in,
        grad_back,
        summed[0],
        summed[1],
        summed[2],
        summed[3],
        summed[4],
        grad_bias_in,
        summed[5],
        summed[6],
        summed[7],
    )


def solution(mesh):
    planes = mesh.shape["fsdp"] // 2
    split = Mesh(mesh.devices.reshape(planes, 2, 2, 2), FSDP_SP)
    rows, flat = P(FSDP, None), P(FSDP)
    both = P(FSDP_SP, None)
    in_specs = (both, flat, rows, rows, rows, rows, *(flat,) * 9, both)
    out_specs = (both, both, rows, rows, rows, rows, *(flat,) * 9)
    return jax.shard_map(body, mesh=split, in_specs=in_specs, out_specs=out_specs, check_vma=False)
```
